32 devices in a mesh: groups: 2 (over y), tm: 4 (over z), batch: 2 (over x), rep: 2 (over core).
Axes of the slice: x: 2, y: 2, z: 4, core: 2. Of those that a mesh axis runs over, the one named last changes fastest.
Arguments:
- latents: bfloat16 [8, 2048, 512], P(('groups', 'batch', 'rep'), 'tm'), parts along dimension 0, may hold values from -6 to 6
- session_ids: int32 [8], P(('groups', 'batch', 'rep')), parts along dimension 0, may hold values from 0 to 7
- session_gain: float32 [8, 512], replicated, may hold values from 0.25 to 1.75
- session_shift: float32 [8, 512], replicated, may hold values from -3 to 3
- first_conv_weight: bfloat16 [3, 512, 512], replicated, may hold values from -0.15625 to 0.15625
- first_conv_bias: float32 [512], replicated, may hold values from -1.5 to 1.5
- second_conv_weight: bfloat16 [3, 512, 512], replicated, may hold values from -0.15625 to 0.15625
- second_conv_bias: float32 [512], replicated, may hold values from -1.5 to 1.5
- proj_weight: bfloat16 [512, 128], replicated, may hold values from -0.25 to 0.25
- offsets: int32 [8, 2048], P(('groups', 'batch', 'rep'), 'tm'), parts along dimension 0, may hold values from 1 to 10
- counts: int32 [8, 4], P(('groups', 'batch', 'rep'), 'tm'), parts along dimension 0, may hold values from 128 to 512, as said below
Outputs:
- embedding: bfloat16 [8, 2048, 128], P(('groups', 'batch', 'rep'), 'tm'), parts along dimension 0
- grad_conv: float32 [6, 512, 512], P('groups', None, 'tm'), parts along dimension 0
- grad_bias: float32 [1024], P(('groups', 'tm')), parts along dimension 0
- grad_proj: float32 [1024, 128], P(('groups', 'tm')), parts along dimension 0
The draws below stay inside these ranges and needn't reach their ends.
There are 2 independent parts, one for each index of `groups`. The reference program is written for one: setup_inputs(seed, part) draws one part's arguments, and reference() takes and returns one part's arrays. A program takes and returns all parts, laid end to end along the dimension named above; an argument that names none is the same for every part. Nothing has to cross between parts.
Inputs may be any that keep to these rules, and one draw needn't show every extreme that they name: `counts`: bin t of a slab is live when t is below the slab's count.
All inputs are finite; a program needn't handle non-finite values.
Results may differ from the reference program's by a relative error of at most 0.0063.
Values may be sent and summed in bfloat16 or wider, within the bound.
A program may use at most 64 MiB of HBM per device.

```python
import jax
import jax.numpy as jnp
from jax import lax

C = 512
EMB = 128
SESS = 8
TBIN = 512
FIRST_DILATION = 1
SECOND_DILATION = 2
OFF_MAX = 10
W = 4
SLABS = 4
WINDOW_BINS = 2048
N_BATCH = 2
N_REP = 2


def draw_session_ids(key, part):
    labels = jax.random.randint(key, (W,), 0, SESS)
    return labels.at[0].set(0).at[W - 1].set(SESS - 1)


def draw_offsets(key, part):
    values = jax.random.randint(key, (W, WINDOW_BINS), 1, OFF_MAX + 1)
    return values.at[0, 0].set(OFF_MAX).at[0, 1].set(1)


def draw_counts(key, part):
    values = jax.random.randint(key, (W, SLABS), TBIN // 4, TBIN + 1)
    return values.at[0, 0].set(TBIN).at[W - 1, SLABS - 1].set(TBIN // 4)


def block_scale(stream_key, dims, pieces, least, high):
    loudness = 1.0
    for position, blocks in pieces:
        draws = jax.random.uniform(jax.random.fold_in(jax.random.fold_in(stream_key, 6), position), (blocks,), jnp.float32, least / len(pieces), high / len(pieces))
        loudness = loudness * jnp.repeat(jnp.exp(draws), dims[position] // blocks).reshape((-1,) + (1,) * (len(dims) - 1 - position))
    return loudness


def scatter_about(key, dims, spread, limit, pieces=(), dtype=jnp.bfloat16):
    factor_of = block_scale(key, dims, pieces, -0.22, 0.18) if pieces else 1.0
    entries = jax.random.normal(key, dims, jnp.float32) * spread * factor_of
    return jnp.minimum(jnp.maximum(entries, -limit), limit).astype(dtype)


def setup_inputs(seed: int = 0, part: int = 0) -> dict:
    keys = jax.random.split(jax.random.key(seed), 12)
    part_keys = jax.random.split(jax.random.fold_in(keys[11], part), 12)
    return {
        "latents": scatter_about(part_keys[0], (W, WINDOW_BINS, C), 1.0, 6.0, ((0, 4), (1, 4))),
        "session_ids": draw_session_ids(jax.random.fold_in(jax.random.fold_in(keys[11], part), 71), part),
        "session_gain": jnp.clip(1.0 + 0.15 * jax.random.normal(keys[2], (SESS, C), jnp.float32), 0.25, 1.75),
        "session_shift": scatter_about(keys[3], (SESS, C), 0.5, 3.0, (), jnp.float32),
        "first_conv_weight": scatter_about(keys[4], (3, C, C), (3 * C) ** -0.5, 0.15625),
        "first_conv_bias": scatter_about(keys[5], (C,), 0.3, 1.5, (), jnp.float32),
        "second_conv_weight": scatter_about(keys[6], (3, C, C), (3 * C) ** -0.5, 0.15625),
        "second_conv_bias": scatter_about(keys[7], (C,), 0.3, 1.5, (), jnp.float32),
        "proj_weight": scatter_about(keys[8], (C, EMB), C ** -0.5, 0.25),
        "offsets": draw_offsets(jax.random.fold_in(jax.random.fold_in(keys[11], part), 71), part),
        "counts": draw_counts(jax.random.fold_in(jax.random.fold_in(keys[11], part), 71), part),
    }


reciprocal_softness = 2.0

def convolved_rows(padded, couple_coefficient, bias, dilation, count):
    total = jnp.zeros((count, couple_coefficient.shape[2]), jnp.float32) + bias[None, :]
    for filter_tap_index in range(3):
        shifted = padded[filter_tap_index * dilation:filter_tap_index * dilation + count]
        total = total + jnp.dot(shifted, couple_coefficient[filter_tap_index], preferred_element_type=jnp.float32)
    return total

def pool_pass(item):
    aggregated_latent_code, aggregated_usable_mask = item
    cosine_affinity_matrix = reciprocal_softness * jnp.dot(aggregated_latent_code, aggregated_latent_code.T, preferred_element_type=jnp.float32)
    count = aggregated_latent_code.shape[0]
    counterpart_latent_code = jnp.arange(count)[:, None] != jnp.arange(count)[None, :]
    couple_coefficient = jnp.where(counterpart_latent_code, jnp.exp(cosine_affinity_matrix - reciprocal_softness), 0.0) * aggregated_usable_mask[None, :]
    denom = lax.optimization_barrier(jnp.sum(couple_coefficient, axis=1))
    soft = (couple_coefficient / denom[:, None]).astype(jnp.bfloat16)
    query_sample_vector = jnp.dot(soft, aggregated_latent_code, preferred_element_type=jnp.float32)
    reverse = (couple_coefficient * aggregated_usable_mask[:, None] / denom[None, :]).astype(jnp.bfloat16)
    aggregated_result = jnp.dot(reverse, aggregated_latent_code, preferred_element_type=jnp.float32)
    return (query_sample_vector, aggregated_result)

def to_pools(values):
    trailing = values.shape[2:]
    grid = values.reshape((N_BATCH, N_REP, SLABS, TBIN) + trailing)
    grid = jnp.moveaxis(grid, 0, 2)
    return grid.reshape((N_REP * SLABS, N_BATCH * TBIN) + trailing)

def from_pools(values):
    trailing = values.shape[2:]
    grid = values.reshape((N_REP, SLABS, N_BATCH, TBIN) + trailing)
    grid = jnp.moveaxis(grid, 2, 0)
    return grid.reshape((W, WINDOW_BINS) + trailing)

def reference(latents, session_ids, session_gain, session_shift, first_conv_weight, first_conv_bias, second_conv_weight, second_conv_bias, proj_weight, offsets, counts):
    gains = session_gain[session_ids][:, None, :]
    shifts = session_shift[session_ids][:, None, :]
    base_offset = (latents.astype(jnp.float32) * gains + shifts).astype(jnp.bfloat16)

    def window_pass(starting_rows):
        input_padded = jnp.pad(starting_rows, ((FIRST_DILATION, FIRST_DILATION), (0, 0)))
        first_preactivation = convolved_rows(input_padded, first_conv_weight, first_conv_bias, FIRST_DILATION, WINDOW_BINS)
        first_hidden = (starting_rows.astype(jnp.float32) + jax.nn.gelu(first_preactivation)).astype(jnp.bfloat16)
        first_padded = jnp.pad(first_hidden, ((SECOND_DILATION, SECOND_DILATION), (0, 0)))
        second_preactivation = convolved_rows(first_padded, second_conv_weight, second_conv_bias, SECOND_DILATION, WINDOW_BINS)
        hidden_two = (first_hidden.astype(jnp.float32) + jax.nn.gelu(second_preactivation)).astype(jnp.bfloat16)
        feats = jnp.dot(hidden_two, proj_weight, preferred_element_type=jnp.float32)
        scale = lax.rsqrt(lax.optimization_barrier(jnp.sum(feats * feats, axis=1)) + 1e-06)
        unit = feats * scale[:, None]
        return (first_padded, second_preactivation, hidden_two, unit, scale)
    first_padded, second_preactivation, hidden_two, unit, scale = lax.map(window_pass, base_offset)
    embed = unit.astype(jnp.bfloat16)
    moment = jnp.arange(WINDOW_BINS)
    usable_mask_vector = ((moment % TBIN)[None, :] < jnp.repeat(counts, TBIN, axis=1)).astype(jnp.float32)
    back_time = moment[None, :] - offsets
    target = jnp.where(back_time >= 0, back_time, moment[None, :] + offsets)
    matched_sample_vector = jnp.take_along_axis(embed, target[:, :, None], axis=1).astype(jnp.float32)
    query_sample_vector, aggregated_result = lax.map(pool_pass, (to_pools(embed), to_pools(usable_mask_vector)))
    query_sample_vector = from_pools(query_sample_vector)
    aggregated_result = from_pools(aggregated_result)

    def push_window(target_row, values):
        return jnp.zeros((WINDOW_BINS, EMB), jnp.float32).at[target_row].add(values)
    propagated_samples = jax.vmap(push_window)(target, usable_mask_vector[:, :, None] * embed.astype(jnp.float32))
    unit_length_derivative = reciprocal_softness * (usable_mask_vector[:, :, None] * (query_sample_vector - matched_sample_vector) + aggregated_result - propagated_samples)
    along = lax.optimization_barrier(jnp.sum(unit * unit_length_derivative, axis=2, keepdims=True))
    grad_feat = ((unit_length_derivative - unit * along) * scale[:, :, None]).astype(jnp.bfloat16)
    grad_proj = jnp.dot(hidden_two.reshape(-1, C).T, grad_feat.reshape(-1, EMB), preferred_element_type=jnp.float32)

    def window_back(carry, item):
        rows_with_padding, pre_rows, feat_rows = item
        grad_hidden = jnp.dot(feat_rows, proj_weight.T, preferred_element_type=jnp.float32)
        unused, pull = jax.vjp(jax.nn.gelu, pre_rows)
        gradient_preactivation = pull(grad_hidden)[0].astype(jnp.bfloat16)
        conv_sum, bias_sum = carry
        filter_taps = jnp.stack([jnp.dot(rows_with_padding[filter_tap_index * SECOND_DILATION:filter_tap_index * SECOND_DILATION + WINDOW_BINS].T, gradient_preactivation, preferred_element_type=jnp.float32) for filter_tap_index in range(3)])
        return ((conv_sum + filter_taps, bias_sum + lax.optimization_barrier(jnp.sum(gradient_preactivation.astype(jnp.float32), axis=0))), None)
    start_carry = (jnp.zeros((3, C, C), jnp.float32), jnp.zeros((C,), jnp.float32))
    (grad_conv, grad_bias), unused_out = lax.scan(window_back, start_carry, (first_padded, second_preactivation, grad_feat))
    return (embed, grad_conv, grad_bias, grad_proj)
```

```python
import functools

import jax
import jax.numpy as jnp
from jax import lax
from jax.experimental import pallas as pl
from jax.experimental.pallas import tpu as pltpu
from jax.sharding import PartitionSpec as P

OFF_MAX = 10
HALO = 16
PAD = 8
LANES = 128
F32 = jnp.float32
BF16 = jnp.bfloat16
GELU_C = 0.7978845608028654
GELU_A = 0.044715


def gelu_parts(x):
    square = x * x
    th = jnp.tanh(GELU_C * x * (1.0 + GELU_A * square))
    half = 0.5 * (1.0 + th)
    slope = half + (0.5 * GELU_C) * x * (1.0 - th * th) * (1.0 + (3.0 * GELU_A) * square)
    return x * half, slope


def kernel(
    n_tm, n_batch, chunks,
    ids_ref, counts_ref, lat_ref, gain_ref, shift_ref, w1_hbm, b1_ref, w2_hbm, b2_ref, proj_ref, off_ref,
    emb_out, conv_out, bias_out, proj_out,
    w1, w2, wsem, halo, meta, meta_next, meta_pool, ext, taps, pre, slope, hid2, unit_s, scale_s, emb_ext, pool,
    xs, rhs, gt, grads, rep_in, part_one, batch_in, part_two, tm_in, final, tmp,
    halo_sem, meta_sem, mpool_sem, pool_sem, rep_sem, batch_sem, tm_sem, gat_sem, fin_sem,
):
    rows, channels = lat_ref.shape
    total = rows + 2 * HALO
    share = channels // n_tm
    piece = share // n_batch
    z = lax.axis_index("tm")
    b = lax.axis_index("batch")
    r = lax.axis_index("rep")
    other = 1 - r
    load1 = pltpu.make_async_copy(w1_hbm, w1, wsem.at[0])
    load2 = pltpu.make_async_copy(w2_hbm, w2, wsem.at[1])
    load1.start()
    load2.start()
    meta[0:1, :] = off_ref[0:1, 0:LANES]
    meta[1:2, :] = jnp.full((1, LANES), counts_ref[0, 0], jnp.int32)
    meta[2:8, :] = jnp.zeros((6, LANES), jnp.int32)

    barrier = pltpu.get_barrier_semaphore()

    def tm_at(o):
        return {"tm": lax.rem(z + o, n_tm)}

    def batch_at(o):
        return {"batch": lax.rem(b + o, n_batch)}

    peers = [tm_at(o) for o in range(1, n_tm)] + [batch_at(o) for o in range(1, n_batch)] + [{"rep": other}]
    for peer in peers:
        pl.semaphore_signal(barrier, inc=1, device_id=peer, device_id_type=pl.DeviceIdType.MESH)
    pl.semaphore_wait(barrier, len(peers))

    started = []

    def send(src, dst, sems, index, peer):
        copy = pltpu.make_async_remote_copy(
            src_ref=src, dst_ref=dst, send_sem=sems.at[(0,) + index], recv_sem=sems.at[(1,) + index],
            device_id=peer, device_id_type=pl.DeviceIdType.MESH,
        )
        copy.start()
        started.append(copy)
        return copy

    low = send(lat_ref.at[pl.ds(rows - HALO, HALO)], halo.at[0], halo_sem, (0,), tm_at(1))
    high = send(lat_ref.at[pl.ds(0, HALO)], halo.at[1], halo_sem, (1,), tm_at(n_tm - 1))
    nextm = send(meta, meta_next, meta_sem, (0,), tm_at(n_tm - 1))
    mpools = [send(meta, meta_pool.at[o - 1], mpool_sem, (o - 1,), batch_at(o)) for o in range(1, n_batch)]

    pick = lax.broadcasted_iota(jnp.int32, gain_ref.shape, 0) == ids_ref[0]
    gain = jnp.sum(jnp.where(pick, gain_ref[...], 0.0), axis=0, keepdims=True)
    shift = jnp.sum(jnp.where(pick, shift_ref[...], 0.0), axis=0, keepdims=True)

    def based(block):
        return (block.astype(F32) * gain + shift).astype(BF16).astype(F32)

    ext[0:PAD, :] = jnp.zeros((PAD, channels), F32)
    ext[PAD + total :, :] = jnp.zeros((PAD, channels), F32)
    ext[PAD + HALO : PAD + HALO + rows, :] = based(lat_ref[...])
    low.wait_recv()
    high.wait_recv()
    has_low = z > 0
    has_high = z < n_tm - 1
    ext[PAD : PAD + HALO, :] = jnp.where(has_low, based(halo[0]), 0.0)
    ext[PAD + HALO + rows : PAD + total, :] = jnp.where(has_high, based(halo[1]), 0.0)

    half = total // 2
    starts = (0, half)

    def gather_taps(dilation):
        for k in range(3):
            first = PAD + (k - 1) * dilation
            taps[:, k * channels : (k + 1) * channels] = ext[first : first + total, :].astype(BF16)

    gather_taps(1)
    load1.wait()
    for s in starts:
        pre[s : s + half, :] = jnp.dot(taps[s : s + half, :], w1[...], preferred_element_type=F32)
    for s in starts:
        x = pre[s : s + half, :] + b1_ref[...]
        value = 0.5 * x * (1.0 + jnp.tanh(GELU_C * x * (1.0 + GELU_A * x * x)))
        hid = (ext[PAD + s : PAD + s + half, :] + value).astype(BF16).astype(F32)
        at = s + lax.broadcasted_iota(jnp.int32, (half, 1), 0)
        inside = jnp.logical_and(
            jnp.logical_or(has_low, at >= HALO), jnp.logical_or(has_high, at < HALO + rows)
        )
        ext[PAD + s : PAD + s + half, :] = jnp.where(inside, hid, 0.0)
    gather_taps(2)
    load2.wait()
    for s in starts:
        pre[s : s + half, :] = jnp.dot(taps[s : s + half, :], w2[...], preferred_element_type=F32)
    for s in starts:
        value, deriv = gelu_parts(pre[s : s + half, :] + b2_ref[...])
        slope[s : s + half, :] = deriv
        hid = (ext[PAD + s : PAD + s + half, :] + value).astype(BF16)
        hid2[s : s + half, :] = hid
        feats = jnp.dot(hid, proj_ref[...], preferred_element_type=F32)
        scale = lax.rsqrt(jnp.sum(feats * feats, axis=1, keepdims=True) + 1e-06)
        unit = feats * scale
        unit_s[s : s + half, :] = unit
        scale_s[s : s + half, :] = jnp.broadcast_to(scale, (half, LANES))
        emb_ext[s : s + half, :] = unit.astype(BF16)
    own = emb_ext[HALO : HALO + rows, :]
    emb_out[...] = own
    pool[0] = own
    pools = [send(pool.at[0], pool.at[o], pool_sem, (o - 1,), batch_at(o)) for o in range(1, n_batch)]

    own_count = meta[1:2, 0:1]
    col = lax.broadcasted_iota(jnp.int32, (rows, 1), 0)
    row = lax.broadcasted_iota(jnp.int32, (1, rows), 1)
    live = (col < own_count).astype(F32)
    first = z * rows
    offs_row = off_ref[...]
    offs_col = jnp.transpose(jnp.broadcast_to(offs_row.astype(F32), (LANES, rows)))[:, 0:1].astype(jnp.int32)
    target_col = jnp.where(first + col - offs_col >= 0, col - offs_col, col + offs_col)
    target_row = jnp.where(first + row - offs_row >= 0, row - offs_row, row + offs_row)
    live_row = (row < own_count).astype(F32)
    band = jnp.where(target_col == row, live, 0.0) + jnp.where(target_row == col, live_row, 0.0)
    paired = jnp.dot(band.astype(BF16), own, preferred_element_type=F32)
    edge = lax.broadcasted_iota(jnp.int32, (1, HALO), 1)
    band_low = jnp.where(target_col == edge - HALO, live, 0.0)
    paired += jnp.dot(band_low.astype(BF16), emb_ext[0:HALO, :], preferred_element_type=F32)
    nextm.wait_recv()
    next_off = meta_next[0:1, 0:HALO]
    next_live = jnp.where(jnp.logical_and(has_high, edge < meta_next[1:2, 0:HALO]), 1.0, 0.0)
    band_high = jnp.where(rows + edge - next_off == col, next_live, 0.0)
    paired += jnp.dot(band_high.astype(BF16), emb_ext[HALO + rows :, :], preferred_element_type=F32)

    for copy in mpools:
        copy.wait_recv()

    def count_of(m):
        return own_count if m == 0 else meta_pool[m - 1, 1:2, 0:1]

    diag = col == row

    def scored(a_block, m):
        s = lax.dot_general(a_block, pool[m], (((1,), (1,)), ((), ())), preferred_element_type=F32)
        return jnp.exp(2.0 * s - 2.0)

    def summed(x, m):
        return jnp.sum(jnp.where(row < count_of(m), x, 0.0), axis=1, keepdims=True)

    x0 = jnp.where(diag, 0.0, scored(own, 0))
    xs[0] = x0.astype(BF16)
    denom = summed(x0, 0)
    for copy in pools:
        copy.wait_recv()
    for m in range(1, n_batch):
        x = scored(own, m)
        xs[m] = x.astype(BF16)
        denom += summed(x, m)

    def set_rhs(a, a_live, a_denom):
        block = pool[a].astype(F32) * a_live
        rhs[a, :, 0:LANES] = block.astype(BF16)
        rhs[a, :, LANES : 2 * LANES] = (block / a_denom).astype(BF16)

    set_rhs(0, live, denom)
    if n_batch == 2:
        other_denom = summed(scored(pool[1], 0), 0)
        other_denom += summed(jnp.where(diag, 0.0, scored(pool[1], 1)), 1)
        set_rhs(1, (col < count_of(1)).astype(F32), other_denom)
    else:
        def one(a, carry):
            block = pool[a]
            den = jnp.zeros((rows, 1), F32)
            for m in range(n_batch):
                den += summed(jnp.where(jnp.logical_and(diag, a == m), 0.0, scored(block, m)), m)
            a_count = meta_pool[a - 1][1:2, 0:1]
            set_rhs(a, (col < a_count).astype(F32), den)
            return carry

        lax.fori_loop(1, n_batch, one, 0)
    acc = jnp.dot(xs[0], rhs[0], preferred_element_type=F32)
    for m in range(1, n_batch):
        acc += jnp.dot(xs[m], rhs[m], preferred_element_type=F32)
    unit = unit_s[HALO : HALO + rows, :]
    scale = scale_s[HALO : HALO + rows, :]
    grad_unit = 2.0 * (live * (acc[:, 0:LANES] / denom + acc[:, LANES:]) - paired)
    along = jnp.sum(unit * grad_unit, axis=1, keepdims=True)
    gf = ((grad_unit - unit * along) * scale).astype(BF16)
    gh = lax.dot_general(gf, proj_ref[...], (((1,), (1,)), ((), ())), preferred_element_type=F32)
    gp = (gh * slope[HALO : HALO + rows, :]).astype(BF16)
    gt[...] = jnp.transpose(gp)

    def put(owner, c, value):
        if piece % 16 == 0:
            grads[owner, c] = jnp.swapaxes(
                value.astype(BF16).reshape(n_tm, n_batch, piece, LANES), 0, 1
            )
        else:
            tmp[...] = value
            for i in range(n_tm):
                for j in range(n_batch):
                    at = i * share + j * piece
                    grads[owner, c, j, i] = tmp[at : at + piece, :].astype(BF16)

    reps = []
    for c in range(chunks):
        if c < chunks - 1:
            value = jnp.dot(
                gt[...], taps[HALO : HALO + rows, 2 * c * LANES : 2 * (c + 1) * LANES], preferred_element_type=F32
            )
            put(0, c, value[:, 0:LANES])
            put(1, c, value[:, LANES:])
        else:
            put(0, c, lax.dot_general(
                hid2[HALO : HALO + rows, :], gf, (((0,), (0,)), ((), ())), preferred_element_type=F32
            ))
            put(1, c, jnp.dot(gt[...], jnp.ones((rows, LANES), BF16), preferred_element_type=F32))
        reps.append(send(grads.at[other, c], rep_in.at[c], rep_sem, (c,), {"rep": other}))

    bats = []
    for c in range(chunks):
        reps[c].wait_recv()
        part_one[c] = (grads[r, c].astype(F32) + rep_in[c].astype(F32)).astype(BF16)
        bats.append([
            send(part_one.at[c, lax.rem(b + o, n_batch)], batch_in.at[c, o - 1], batch_sem, (c, o - 1), batch_at(o))
            for o in range(1, n_batch)
        ])
    tms = []
    for c in range(chunks):
        value = part_one[c, b].astype(F32)
        for o in range(1, n_batch):
            bats[c][o - 1].wait_recv()
            value += batch_in[c, o - 1].astype(F32)
        part_two[c] = value.astype(BF16)
        tms.append([
            send(part_two.at[c, lax.rem(z + o, n_tm)], tm_in.at[c, o - 1], tm_sem, (c, o - 1), tm_at(o))
            for o in range(1, n_tm)
        ])
    gats = []
    for c in range(chunks):
        value = part_two[c, z].astype(F32)
        for o in range(1, n_tm):
            tms[c][o - 1].wait_recv()
            value += tm_in[c, o - 1].astype(F32)
        final[r, c, b] = value.astype(BF16)
        gats.append([
            send(final.at[r, c, b], final.at[r, c, b], gat_sem, (c, o - 1), batch_at(o)) for o in range(1, n_batch)
        ])
    fins = []
    for c in range(chunks):
        for copy in gats[c]:
            copy.wait_recv()
        fins.append(send(final.at[r, c], final.at[r, c], fin_sem, (c,), {"rep": other}))
    per_tap = channels // LANES
    for c in range(chunks):
        fins[c].wait_recv()
        for owner in range(2):
            if piece % 16 == 0:
                value = final[owner, c].astype(F32).reshape(share, LANES)
            else:
                for j in range(n_batch):
                    tmp[j * piece : (j + 1) * piece, :] = final[owner, c, j].astype(F32)
                value = tmp[0:share, :]
            chunk = 2 * c + owner
            if c < chunks - 1:
                k, part = divmod(chunk, per_tap)
                conv_out[k, part * LANES : (part + 1) * LANES, :] = jnp.transpose(value)
            elif owner == 0:
                proj_out[...] = value
            else:
                bias_out[...] = jnp.transpose(value)[0:1, :]
    for copy in started:
        copy.wait_send()


def per_device(
    n_tm, n_batch,
    latents, session_ids, session_gain, session_shift, first_conv_weight, first_conv_bias,
    second_conv_weight, second_conv_bias, proj_weight, offsets, counts,
):
    rows, channels = latents.shape[1:]
    emb = proj_weight.shape[1]
    total = rows + 2 * HALO
    share = channels // n_tm
    piece = share // n_batch
    chunks = (3 * channels // LANES + 2) // 2
    vmem = pl.BlockSpec(memory_space=pltpu.VMEM)
    smem = pl.BlockSpec(memory_space=pltpu.SMEM)
    hbm = pl.BlockSpec(memory_space=pl.ANY)
    nb = n_batch - 1
    dma = pltpu.SemaphoreType.DMA
    embed, conv, bias, proj = pl.pallas_call(
        functools.partial(kernel, n_tm, n_batch, chunks),
        out_shape=(
            jax.ShapeDtypeStruct((rows, emb), BF16),
            jax.ShapeDtypeStruct((3, channels, share), F32),
            jax.ShapeDtypeStruct((1, share), F32),
            jax.ShapeDtypeStruct((share, emb), F32),
        ),
        in_specs=[smem, smem, vmem, vmem, vmem, hbm, vmem, hbm, vmem, vmem, vmem],
        out_specs=(vmem, vmem, vmem, vmem),
        scratch_shapes=[
            pltpu.VMEM((3 * channels, channels), BF16),
            pltpu.VMEM((3 * channels, channels), BF16),
            dma((2,)),
            pltpu.VMEM((2, HALO, channels), BF16),
            pltpu.VMEM((8, LANES), jnp.int32),
            pltpu.VMEM((8, LANES), jnp.int32),
            pltpu.VMEM((nb, 8, LANES), jnp.int32),
            pltpu.VMEM((total + 2 * PAD, channels), F32),
            pltpu.VMEM((total, 3 * channels), BF16),
            pltpu.VMEM((total, channels), F32),
            pltpu.VMEM((total, channels), F32),
            pltpu.VMEM((total, channels), BF16),
            pltpu.VMEM((total, emb), F32),
            pltpu.VMEM((total, LANES), F32),
            pltpu.VMEM((total, emb), BF16),
            pltpu.VMEM((n_batch, rows, emb), BF16),
            pltpu.VMEM((n_batch, rows, rows), BF16),
            pltpu.VMEM((n_batch, rows, 2 * emb), BF16),
            pltpu.VMEM((channels, rows), BF16),
            pltpu.VMEM((2, chunks, n_batch, n_tm, piece, LANES), BF16),
            pltpu.VMEM((chunks, n_batch, n_tm, piece, LANES), BF16),
            pltpu.VMEM((chunks, n_batch, n_tm, piece, LANES), BF16),
            pltpu.VMEM((chunks, nb, n_tm, piece, LANES), BF16),
            pltpu.VMEM((chunks, n_tm, piece, LANES), BF16),
            pltpu.VMEM((chunks, n_tm - 1, piece, LANES), BF16),
            pltpu.VMEM((2, chunks, n_batch, piece, LANES), BF16),
            pltpu.VMEM((channels, LANES), F32),
            dma((2, 2)),
            dma((2, 1)),
            dma((2, nb)),
            dma((2, nb)),
            dma((2, chunks)),
            dma((2, chunks, nb)),
            dma((2, chunks, n_tm - 1)),
            dma((2, chunks, nb)),
            dma((2, chunks)),
        ],
        compiler_params=pltpu.CompilerParams(
            collective_id=0, has_side_effects=True, vmem_limit_bytes=56 * 1024 * 1024
        ),
    )(
        session_ids, counts, latents[0], session_gain, session_shift,
        first_conv_weight.reshape(3 * channels, channels), first_conv_bias[None],
        second_conv_weight.reshape(3 * channels, channels), second_conv_bias[None],
        proj_weight, offsets,
    )
    return embed[None], conv, bias[0], proj


def solution(mesh):
    return jax.shard_map(
        functools.partial(per_device, mesh.shape["tm"], mesh.shape["batch"]),
        mesh=mesh,
        in_specs=(
            P(("groups", "batch", "rep"), "tm", None),
            P(("groups", "batch", "rep")),
            P(),
            P(),
            P(),
            P(),
            P(),
            P(),
            P(),
            P(("groups", "batch", "rep"), "tm"),
            P(("groups", "batch", "rep"), "tm"),
        ),
        out_specs=(
            P(("groups", "batch", "rep"), "tm", None),
            P("groups", None, "tm"),
            P(("groups", "tm")),
            P(("groups", "tm"), None),
        ),
        check_vma=False,
    )
```

```python
import functools

import jax
import jax.numpy as jnp
from jax import lax
from jax.experimental import pallas as pl
from jax.experimental.pallas import tpu as pltpu
from jax.sharding import PartitionSpec as P

OFF_MAX = 10
HALO = 16
PAD = 8
LANES = 128
F32 = jnp.float32
BF16 = jnp.bfloat16
GELU_C = 0.7978845608028654
GELU_A = 0.044715


def gelu_parts(x):
    square = x * x
    th = jnp.tanh(GELU_C * x * (1.0 + GELU_A * square))
    half = 0.5 * (1.0 + th)
    slope = half + (0.5 * GELU_C) * x * (1.0 - th * th) * (1.0 + (3.0 * GELU_A) * square)
    return x * half, slope


def kernel(
    n_tm, n_batch, chunks,
    ids_ref, counts_ref, lat_ref, gain_ref, shift_ref, w1_hbm, b1_ref, w2_hbm, b2_ref, proj_ref, off_ref,
    emb_out, sums_out,
    w1, w2, wsem, halo, meta, meta_next, meta_pool, ext, taps, pre, slope, hid2, unit_s, scale_s, emb_ext, pool,
    xs, rhs, gt, grads, rep_in, part_one, batch_in, part_two, tm_in, final, tmp,
    halo_sem, meta_sem, mpool_sem, pool_sem, rep_sem, batch_sem, tm_sem, gat_sem, fin_sem,
):
    rows, channels = lat_ref.shape
    total = rows + 2 * HALO
    share = channels // n_tm
    piece = share // n_batch
    z = lax.axis_index("tm")
    b = lax.axis_index("batch")
    r = lax.axis_index("rep")
    other = 1 - r
    load1 = pltpu.make_async_copy(w1_hbm, w1, wsem.at[0])
    load2 = pltpu.make_async_copy(w2_hbm, w2, wsem.at[1])
    load1.start()
    load2.start()
    meta[0:1, :] = off_ref[0:1, 0:LANES]
    meta[1:2, :] = jnp.broadcast_to(counts_ref[...], (1, LANES))
    meta[2:8, :] = jnp.zeros((6, LANES), jnp.int32)

    barrier = pltpu.get_barrier_semaphore()

    def tm_at(o):
        return {"tm": lax.rem(z + o, n_tm)}

    def batch_at(o):
        return {"batch": lax.rem(b + o, n_batch)}

    peers = [tm_at(o) for o in range(1, n_tm)] + [batch_at(o) for o in range(1, n_batch)] + [{"rep": other}]
    for peer in peers:
        pl.semaphore_signal(barrier, inc=1, device_id=peer, device_id_type=pl.DeviceIdType.MESH)
    pl.semaphore_wait(barrier, len(peers))

    started = []

    def send(src, dst, sems, index, peer):
        copy = pltpu.make_async_remote_copy(
            src_ref=src, dst_ref=dst, send_sem=sems.at[(0,) + index], recv_sem=sems.at[(1,) + index],
            device_id=peer, device_id_type=pl.DeviceIdType.MESH,
        )
        copy.start()
        started.append(copy)
        return copy

    low = send(lat_ref.at[pl.ds(rows - HALO, HALO)], halo.at[0], halo_sem, (0,), tm_at(1))
    high = send(lat_ref.at[pl.ds(0, HALO)], halo.at[1], halo_sem, (1,), tm_at(n_tm - 1))
    nextm = send(meta, meta_next, meta_sem, (0,), tm_at(n_tm - 1))
    mpools = [send(meta, meta_pool.at[o - 1], mpool_sem, (o - 1,), batch_at(o)) for o in range(1, n_batch)]

    pick = lax.broadcasted_iota(jnp.int32, gain_ref.shape, 0) == ids_ref[...]
    gain = jnp.sum(jnp.where(pick, gain_ref[...], 0.0), axis=0, keepdims=True)
    shift = jnp.sum(jnp.where(pick, shift_ref[...], 0.0), axis=0, keepdims=True)

    def based(block):
        return (block.astype(F32) * gain + shift).astype(BF16).astype(F32)

    ext[0:PAD, :] = jnp.zeros((PAD, channels), F32)
    ext[PAD + total :, :] = jnp.zeros((PAD, channels), F32)
    ext[PAD + HALO : PAD + HALO + rows, :] = based(lat_ref[...])
    ext[PAD : PAD + HALO, :] = jnp.zeros((HALO, channels), F32)
    ext[PAD + HALO + rows : PAD + total, :] = jnp.zeros((HALO, channels), F32)
    has_low = z > 0
    has_high = z < n_tm - 1
    half = total // 2
    starts = (0, half)
    edge_rows = 2 * HALO
    middle = total - 2 * edge_rows

    def gather_taps(dilation, begin, count):
        for k in range(3):
            first = PAD + begin + (k - 1) * dilation
            taps[begin : begin + count, k * channels : (k + 1) * channels] = ext[first : first + count, :].astype(BF16)

    def first_hidden(begin, count):
        x = pre[begin : begin + count, :] + b1_ref[...]
        value = 0.5 * x * (1.0 + jnp.tanh(GELU_C * x * (1.0 + GELU_A * x * x)))
        hid = (ext[PAD + begin : PAD + begin + count, :] + value).astype(BF16).astype(F32)
        at = begin + lax.broadcasted_iota(jnp.int32, (count, 1), 0)
        inside = jnp.logical_and(
            jnp.logical_or(has_low, at >= HALO), jnp.logical_or(has_high, at < HALO + rows)
        )
        return jnp.where(inside, hid, 0.0)

    gather_taps(1, edge_rows, middle)
    load1.wait()
    pre[edge_rows : edge_rows + middle, :] = jnp.dot(
        taps[edge_rows : edge_rows + middle, :], w1[...], preferred_element_type=F32
    )
    low.wait_recv()
    high.wait_recv()
    ext[PAD : PAD + HALO, :] = jnp.where(has_low, based(halo[0]), 0.0)
    ext[PAD + HALO + rows : PAD + total, :] = jnp.where(has_high, based(halo[1]), 0.0)
    last = total - edge_rows
    gather_taps(1, 0, edge_rows)
    gather_taps(1, last, edge_rows)
    ends = jnp.concatenate([taps[0:edge_rows, :], taps[last:, :]], axis=0)
    ends = jnp.dot(ends, w1[...], preferred_element_type=F32)
    pre[0:edge_rows, :] = ends[0:edge_rows, :]
    pre[last:, :] = ends[edge_rows:, :]
    for s in starts:
        ext[PAD + s : PAD + s + half, :] = first_hidden(s, half)
    gather_taps(2, 0, total)
    load2.wait()
    for s in starts:
        pre[s : s + half, :] = jnp.dot(taps[s : s + half, :], w2[...], preferred_element_type=F32)
    for s in starts:
        value, deriv = gelu_parts(pre[s : s + half, :] + b2_ref[...])
        slope[s : s + half, :] = deriv
        hid = (ext[PAD + s : PAD + s + half, :] + value).astype(BF16)
        hid2[s : s + half, :] = hid
        feats = jnp.dot(hid, proj_ref[...], preferred_element_type=F32)
        scale = lax.rsqrt(jnp.sum(feats * feats, axis=1, keepdims=True) + 1e-06)
        unit = feats * scale
        unit_s[s : s + half, :] = unit
        scale_s[s : s + half, :] = jnp.broadcast_to(scale, (half, LANES))
        emb_ext[s : s + half, :] = unit.astype(BF16)
    own = emb_ext[HALO : HALO + rows, :]
    emb_out[...] = own
    pool[0] = own
    pools = [send(pool.at[0], pool.at[o], pool_sem, (o - 1,), batch_at(o)) for o in range(1, n_batch)]

    own_count = meta[1:2, 0:1]
    col = lax.broadcasted_iota(jnp.int32, (rows, 1), 0)
    row = lax.broadcasted_iota(jnp.int32, (1, rows), 1)
    live = (col < own_count).astype(F32)
    first = z * rows
    offs_row = off_ref[...]
    offs_col = jnp.transpose(jnp.broadcast_to(offs_row.astype(F32), (LANES, rows)))[:, 0:1].astype(jnp.int32)
    target_col = jnp.where(first + col - offs_col >= 0, col - offs_col, col + offs_col)
    target_row = jnp.where(first + row - offs_row >= 0, row - offs_row, row + offs_row)
    live_row = (row < own_count).astype(F32)
    band = jnp.where(target_col == row, live, 0.0) + jnp.where(target_row == col, live_row, 0.0)
    paired = jnp.dot(band.astype(BF16), own, preferred_element_type=F32)
    edge = lax.broadcasted_iota(jnp.int32, (1, HALO), 1)
    band_low = jnp.where(target_col == edge - HALO, live, 0.0)
    paired += jnp.dot(band_low.astype(BF16), emb_ext[0:HALO, :], preferred_element_type=F32)
    nextm.wait_recv()
    next_off = meta_next[0:1, 0:HALO]
    next_live = jnp.where(jnp.logical_and(has_high, edge < meta_next[1:2, 0:HALO]), 1.0, 0.0)
    band_high = jnp.where(rows + edge - next_off == col, next_live, 0.0)
    paired += jnp.dot(band_high.astype(BF16), emb_ext[HALO + rows :, :], preferred_element_type=F32)

    for copy in mpools:
        copy.wait_recv()

    def count_of(m):
        return own_count if m == 0 else meta_pool[m - 1, 1:2, 0:1]

    diag = col == row

    def scored(a_block, m):
        s = lax.dot_general(a_block, pool[m], (((1,), (1,)), ((), ())), preferred_element_type=F32)
        return jnp.exp(2.0 * s - 2.0)

    def summed(x, m):
        return jnp.sum(jnp.where(row < count_of(m), x, 0.0), axis=1, keepdims=True)

    x0 = jnp.where(diag, 0.0, scored(own, 0))
    xs[0] = x0.astype(BF16)
    denom = summed(x0, 0)
    for copy in pools:
        copy.wait_recv()
    for m in range(1, n_batch):
        x = scored(own, m)
        xs[m] = x.astype(BF16)
        denom += summed(x, m)

    def set_rhs(a, a_live, a_denom):
        block = pool[a].astype(F32) * a_live
        rhs[a, :, 0:LANES] = block.astype(BF16)
        rhs[a, :, LANES : 2 * LANES] = (block / a_denom).astype(BF16)

    set_rhs(0, live, denom)
    if n_batch == 2:
        other_denom = summed(scored(pool[1], 0), 0)
        other_denom += summed(jnp.where(diag, 0.0, scored(pool[1], 1)), 1)
        set_rhs(1, (col < count_of(1)).astype(F32), other_denom)
    else:
        def one(a, carry):
            block = pool[a]
            den = jnp.zeros((rows, 1), F32)
            for m in range(n_batch):
                den += summed(jnp.where(jnp.logical_and(diag, a == m), 0.0, scored(block, m)), m)
            a_count = meta_pool[a - 1][1:2, 0:1]
            set_rhs(a, (col < a_count).astype(F32), den)
            return carry

        lax.fori_loop(1, n_batch, one, 0)
    acc = jnp.dot(xs[0], rhs[0], preferred_element_type=F32)
    for m in range(1, n_batch):
        acc += jnp.dot(xs[m], rhs[m], preferred_element_type=F32)
    unit = unit_s[HALO : HALO + rows, :]
    scale = scale_s[HALO : HALO + rows, :]
    grad_unit = 2.0 * (live * (acc[:, 0:LANES] / denom + acc[:, LANES:]) - paired)
    along = jnp.sum(unit * grad_unit, axis=1, keepdims=True)
    gf = ((grad_unit - unit * along) * scale).astype(BF16)
    gh = lax.dot_general(gf, proj_ref[...], (((1,), (1,)), ((), ())), preferred_element_type=F32)
    gp = (gh * slope[HALO : HALO + rows, :]).astype(BF16)
    gt[...] = jnp.transpose(gp)

    def put(owner, c, value):
        if piece % 16 == 0:
            grads[owner, c] = jnp.swapaxes(
                value.astype(BF16).reshape(n_tm, n_batch, piece, LANES), 0, 1
            )
        else:
            tmp[...] = value
            for i in range(n_tm):
                for j in range(n_batch):
                    at = i * share + j * piece
                    grads[owner, c, j, i] = tmp[at : at + piece, :].astype(BF16)

    reps = {}

    def produce(c):
        if c < chunks - 1:
            value = jnp.dot(
                gt[...], taps[HALO : HALO + rows, 2 * c * LANES : 2 * (c + 1) * LANES], preferred_element_type=F32
            )
            put(0, c, value[:, 0:LANES])
            put(1, c, value[:, LANES:])
        else:
            put(0, c, lax.dot_general(
                hid2[HALO : HALO + rows, :], gf, (((0,), (0,)), ((), ())), preferred_element_type=F32
            ))
            put(1, c, jnp.dot(gt[...], jnp.ones((rows, LANES), BF16), preferred_element_type=F32))
        reps[c] = send(grads.at[other, c], rep_in.at[c], rep_sem, (c,), {"rep": other})

    bats, tms, gats, fins = {}, {}, {}, {}

    def over_batch(c):
        reps[c].wait_recv()
        part_one[c] = (grads[r, c].astype(F32) + rep_in[c].astype(F32)).astype(BF16)
        bats[c] = [
            send(part_one.at[c, lax.rem(b + o, n_batch)], batch_in.at[c, o - 1], batch_sem, (c, o - 1), batch_at(o))
            for o in range(1, n_batch)
        ]

    def over_tm(c):
        value = part_one[c, b].astype(F32)
        for o in range(1, n_batch):
            bats[c][o - 1].wait_recv()
            value += batch_in[c, o - 1].astype(F32)
        part_two[c] = value.astype(BF16)
        tms[c] = [
            send(part_two.at[c, lax.rem(z + o, n_tm)], tm_in.at[c, o - 1], tm_sem, (c, o - 1), tm_at(o))
            for o in range(1, n_tm)
        ]

    def finish(c):
        value = part_two[c, z].astype(F32)
        for o in range(1, n_tm):
            tms[c][o - 1].wait_recv()
            value += tm_in[c, o - 1].astype(F32)
        final[r, c, b] = value.astype(BF16)
        gats[c] = [
            send(final.at[r, c, b], final.at[r, c, b], gat_sem, (c, o - 1), batch_at(o)) for o in range(1, n_batch)
        ]

    def share_out(c):
        for copy in gats[c]:
            copy.wait_recv()
        fins[c] = send(final.at[r, c], final.at[r, c], fin_sem, (c,), {"rep": other})

    def write(c):
        fins[c].wait_recv()
        for owner in range(2):
            sums_out[owner, c] = final[owner, c]

    for c in range(chunks):
        produce(c)
        if c >= 1:
            over_batch(c - 1)
    over_batch(chunks - 1)
    for step in range(chunks + 4):
        for lag, stage in ((4, write), (3, share_out), (2, finish), (0, over_tm)):
            if 0 <= step - lag < chunks:
                stage(step - lag)
    for copy in started:
        copy.wait_send()


def spread(emb_ref, sums_ref, emb_out, conv_out, bias_out, proj_out, tmp):
    chunks, n_batch, piece = sums_ref.shape[1:4]
    per_tap = conv_out.shape[1] // LANES
    share = n_batch * piece
    emb_out[...] = emb_ref[...]
    for c in range(chunks):
        for owner in range(2):
            if piece % 16 == 0:
                value = sums_ref[owner, c].astype(F32).reshape(share, LANES)
            else:
                for j in range(n_batch):
                    tmp[j * piece : (j + 1) * piece, :] = sums_ref[owner, c, j].astype(F32)
                value = tmp[...]
            if c < chunks - 1:
                k, part = divmod(2 * c + owner, per_tap)
                conv_out[k, part * LANES : (part + 1) * LANES, :] = jnp.transpose(value)
            elif owner == 0:
                proj_out[...] = value
            else:
                bias_out[...] = jnp.transpose(value)[0:1, :]


def per_device(
    n_tm, n_batch,
    latents, session_ids, session_gain, session_shift, first_conv_weight, first_conv_bias,
    second_conv_weight, second_conv_bias, proj_weight, offsets, counts,
):
    rows, channels = latents.shape[1:]
    emb = proj_weight.shape[1]
    total = rows + 2 * HALO
    share = channels // n_tm
    piece = share // n_batch
    chunks = (3 * channels // LANES + 2) // 2
    vmem = pl.BlockSpec(memory_space=pltpu.VMEM)
    hbm = pl.BlockSpec(memory_space=pl.ANY)
    nb = n_batch - 1
    dma = pltpu.SemaphoreType.DMA
    embed, sums = pl.pallas_call(
        functools.partial(kernel, n_tm, n_batch, chunks),
        out_shape=(
            jax.ShapeDtypeStruct((rows, emb), BF16),
            jax.ShapeDtypeStruct((2, chunks, n_batch, piece, LANES), BF16),
        ),
        in_specs=[vmem, vmem, vmem, vmem, vmem, hbm, vmem, hbm, vmem, vmem, vmem],
        out_specs=(vmem, vmem),
        scratch_shapes=[
            pltpu.VMEM((3 * channels, channels), BF16),
            pltpu.VMEM((3 * channels, channels), BF16),
            dma((2,)),
            pltpu.VMEM((2, HALO, channels), BF16),
            pltpu.VMEM((8, LANES), jnp.int32),
            pltpu.VMEM((8, LANES), jnp.int32),
            pltpu.VMEM((nb, 8, LANES), jnp.int32),
            pltpu.VMEM((total + 2 * PAD, channels), F32),
            pltpu.VMEM((total, 3 * channels), BF16),
            pltpu.VMEM((total, channels), F32),
            pltpu.VMEM((total, channels), F32),
            pltpu.VMEM((total, channels), BF16),
            pltpu.VMEM((total, emb), F32),
            pltpu.VMEM((total, LANES), F32),
            pltpu.VMEM((total, emb), BF16),
            pltpu.VMEM((n_batch, rows, emb), BF16),
            pltpu.VMEM((n_batch, rows, rows), BF16),
            pltpu.VMEM((n_batch, rows, 2 * emb), BF16),
            pltpu.VMEM((channels, rows), BF16),
            pltpu.VMEM((2, chunks, n_batch, n_tm, piece, LANES), BF16),
            pltpu.VMEM((chunks, n_batch, n_tm, piece, LANES), BF16),
            pltpu.VMEM((chunks, n_batch, n_tm, piece, LANES), BF16),
            pltpu.VMEM((chunks, nb, n_tm, piece, LANES), BF16),
            pltpu.VMEM((chunks, n_tm, piece, LANES), BF16),
            pltpu.VMEM((chunks, n_tm - 1, piece, LANES), BF16),
            pltpu.VMEM((2, chunks, n_batch, piece, LANES), BF16),
            pltpu.VMEM((channels, LANES), F32),
            dma((2, 2)),
            dma((2, 1)),
            dma((2, nb)),
            dma((2, nb)),
            dma((2, chunks)),
            dma((2, chunks, nb)),
            dma((2, chunks, n_tm - 1)),
            dma((2, chunks, nb)),
            dma((2, chunks)),
        ],
        compiler_params=pltpu.CompilerParams(
            collective_id=0, has_side_effects=True, vmem_limit_bytes=56 * 1024 * 1024
        ),
    )(
        session_ids[None], counts, latents[0], session_gain, session_shift,
        first_conv_weight.reshape(3 * channels, channels), first_conv_bias[None],
        second_conv_weight.reshape(3 * channels, channels), second_conv_bias[None],
        proj_weight, offsets,
    )
    embed, conv, bias, proj = pl.pallas_call(
        spread,
        out_shape=(
            jax.ShapeDtypeStruct((rows, emb), BF16),
            jax.ShapeDtypeStruct((3, channels, share), F32),
            jax.ShapeDtypeStruct((1, share), F32),
            jax.ShapeDtypeStruct((share, emb), F32),
        ),
        in_specs=[vmem, vmem],
        out_specs=(vmem, vmem, vmem, vmem),
        scratch_shapes=[pltpu.VMEM((share, LANES), F32)],
    )(embed, sums)
    return embed[None], conv, bias[0], proj


def solution(mesh):
    return jax.shard_map(
        functools.partial(per_device, mesh.shape["tm"], mesh.shape["batch"]),
        mesh=mesh,
        in_specs=(
            P(("groups", "batch", "rep"), "tm", None),
            P(("groups", "batch", "rep")),
            P(),
            P(),
            P(),
            P(),
            P(),
            P(),
            P(),
            P(("groups", "batch", "rep"), "tm"),
            P(("groups", "batch", "rep"), "tm"),
        ),
        out_specs=(
            P(("groups", "batch", "rep"), "tm", None),
            P("groups", None, "tm"),
            P(("groups", "tm")),
            P(("groups", "tm"), None),
        ),
        check_vma=False,
    )
```

```python
import functools

import jax
import jax.numpy as jnp
from jax import lax
from jax.experimental import pallas as pl
from jax.experimental.pallas import tpu as pltpu
from jax.sharding import PartitionSpec as P

OFF_MAX = 10
HALO = 16
PAD = 8
LANES = 128
F32 = jnp.float32
BF16 = jnp.bfloat16
GELU_C = 0.7978845608028654
GELU_A = 0.044715


def gelu_parts(x):
    square = x * x
    th = jnp.tanh(GELU_C * x * (1.0 + GELU_A * square))
    half = 0.5 * (1.0 + th)
    slope = half + (0.5 * GELU_C) * x * (1.0 - th * th) * (1.0 + (3.0 * GELU_A) * square)
    return x * half, slope


def kernel(
    n_tm, n_batch, chunks,
    id_count_ref, lat_ref, gain_ref, shift_ref, w1_hbm, b1_ref, w2_hbm, b2_ref, proj_ref, off_ref,
    emb_out, sums_out,
    w1, w2, wsem, halo, meta, meta_next, meta_pool, ext, taps, pre, slope, hid2, unit_s, scale_s, emb_ext, pool,
    xs, rhs, gt, grads, rep_in, part_one, batch_in, part_two, tm_in, final, tmp,
    halo_sem, meta_sem, mpool_sem, pool_sem, rep_sem, batch_sem, tm_sem, gat_sem, fin_sem,
):
    rows, channels = lat_ref.shape
    total = rows + 2 * HALO
    share = channels // n_tm
    piece = share // n_batch
    z = lax.axis_index("tm")
    b = lax.axis_index("batch")
    r = lax.axis_index("rep")
    other = 1 - r
    load1 = pltpu.make_async_copy(w1_hbm, w1, wsem.at[0])
    load2 = pltpu.make_async_copy(w2_hbm, w2, wsem.at[1])
    load1.start()
    load2.start()
    meta[0:1, :] = off_ref[0:1, 0:LANES]
    meta[1:2, :] = id_count_ref[1:2, :]
    meta[2:8, :] = jnp.zeros((6, LANES), jnp.int32)

    barrier = pltpu.get_barrier_semaphore()

    def tm_at(o):
        return {"tm": lax.rem(z + o, n_tm)}

    def batch_at(o):
        return {"batch": lax.rem(b + o, n_batch)}

    peers = [tm_at(o) for o in range(1, n_tm)] + [batch_at(o) for o in range(1, n_batch)] + [{"rep": other}]
    for peer in peers:
        pl.semaphore_signal(barrier, inc=1, device_id=peer, device_id_type=pl.DeviceIdType.MESH)
    pl.semaphore_wait(barrier, len(peers))

    started = []

    def send(src, dst, sems, index, peer):
        copy = pltpu.make_async_remote_copy(
            src_ref=src, dst_ref=dst, send_sem=sems.at[(0,) + index], recv_sem=sems.at[(1,) + index],
            device_id=peer, device_id_type=pl.DeviceIdType.MESH,
        )
        copy.start()
        started.append(copy)
        return copy

    low = send(lat_ref.at[pl.ds(rows - HALO, HALO)], halo.at[0], halo_sem, (0,), tm_at(1))
    high = send(lat_ref.at[pl.ds(0, HALO)], halo.at[1], halo_sem, (1,), tm_at(n_tm - 1))
    nextm = send(meta, meta_next, meta_sem, (0,), tm_at(n_tm - 1))
    mpools = [send(meta, meta_pool.at[o - 1], mpool_sem, (o - 1,), batch_at(o)) for o in range(1, n_batch)]

    pick = lax.broadcasted_iota(jnp.int32, gain_ref.shape, 0) == id_count_ref[0:1, 0:1]
    gain = jnp.sum(jnp.where(pick, gain_ref[...], 0.0), axis=0, keepdims=True)
    shift = jnp.sum(jnp.where(pick, shift_ref[...], 0.0), axis=0, keepdims=True)

    def based(block):
        return (block.astype(F32) * gain + shift).astype(BF16).astype(F32)

    ext[0:PAD, :] = jnp.zeros((PAD, channels), F32)
    ext[PAD + total :, :] = jnp.zeros((PAD, channels), F32)
    ext[PAD + HALO : PAD + HALO + rows, :] = based(lat_ref[...])
    ext[PAD : PAD + HALO, :] = jnp.zeros((HALO, channels), F32)
    ext[PAD + HALO + rows : PAD + total, :] = jnp.zeros((HALO, channels), F32)
    has_low = z > 0
    has_high = z < n_tm - 1
    half = total // 2
    starts = (0, half)
    edge_rows = 2 * HALO
    middle = total - 2 * edge_rows

    def gather_taps(dilation, begin, count):
        for k in range(3):
            first = PAD + begin + (k - 1) * dilation
            taps[begin : begin + count, k * channels : (k + 1) * channels] = ext[first : first + count, :].astype(BF16)

    def first_hidden(begin, count):
        x = pre[begin : begin + count, :] + b1_ref[...]
        value = 0.5 * x * (1.0 + jnp.tanh(GELU_C * x * (1.0 + GELU_A * x * x)))
        hid = (ext[PAD + begin : PAD + begin + count, :] + value).astype(BF16).astype(F32)
        at = begin + lax.broadcasted_iota(jnp.int32, (count, 1), 0)
        inside = jnp.logical_and(
            jnp.logical_or(has_low, at >= HALO), jnp.logical_or(has_high, at < HALO + rows)
        )
        return jnp.where(inside, hid, 0.0)

    gather_taps(1, edge_rows, middle)
    load1.wait()
    pre[edge_rows : edge_rows + middle, :] = jnp.dot(
        taps[edge_rows : edge_rows + middle, :], w1[...], preferred_element_type=F32
    )
    low.wait_recv()
    high.wait_recv()
    ext[PAD : PAD + HALO, :] = jnp.where(has_low, based(halo[0]), 0.0)
    ext[PAD + HALO + rows : PAD + total, :] = jnp.where(has_high, based(halo[1]), 0.0)
    last = total - edge_rows
    gather_taps(1, 0, edge_rows)
    gather_taps(1, last, edge_rows)
    ends = jnp.concatenate([taps[0:edge_rows, :], taps[last:, :]], axis=0)
    ends = jnp.dot(ends, w1[...], preferred_element_type=F32)
    pre[0:edge_rows, :] = ends[0:edge_rows, :]
    pre[last:, :] = ends[edge_rows:, :]
    for s in starts:
        ext[PAD + s : PAD + s + half, :] = first_hidden(s, half)
    gather_taps(2, 0, total)
    load2.wait()
    for s in starts:
        pre[s : s + half, :] = jnp.dot(taps[s : s + half, :], w2[...], preferred_element_type=F32)
    for s in starts:
        value, deriv = gelu_parts(pre[s : s + half, :] + b2_ref[...])
        slope[s : s + half, :] = deriv
        hid = (ext[PAD + s : PAD + s + half, :] + value).astype(BF16)
        hid2[s : s + half, :] = hid
        feats = jnp.dot(hid, proj_ref[...], preferred_element_type=F32)
        scale = lax.rsqrt(jnp.sum(feats * feats, axis=1, keepdims=True) + 1e-06)
        unit = feats * scale
        unit_s[s : s + half, :] = unit
        scale_s[s : s + half, :] = jnp.broadcast_to(scale, (half, LANES))
        emb_ext[s : s + half, :] = unit.astype(BF16)
    own = emb_ext[HALO : HALO + rows, :]
    emb_out[...] = own
    pool[0] = own
    pools = [send(pool.at[0], pool.at[o], pool_sem, (o - 1,), batch_at(o)) for o in range(1, n_batch)]

    own_count = meta[1:2, 0:1]
    col = lax.broadcasted_iota(jnp.int32, (rows, 1), 0)
    row = lax.broadcasted_iota(jnp.int32, (1, rows), 1)
    live = (col < own_count).astype(F32)
    first = z * rows
    offs_row = off_ref[...]
    offs_col = jnp.transpose(jnp.broadcast_to(offs_row.astype(F32), (LANES, rows)))[:, 0:1].astype(jnp.int32)
    target_col = jnp.where(first + col - offs_col >= 0, col - offs_col, col + offs_col)
    target_row = jnp.where(first + row - offs_row >= 0, row - offs_row, row + offs_row)
    live_row = (row < own_count).astype(F32)
    band = jnp.where(target_col == row, live, 0.0) + jnp.where(target_row == col, live_row, 0.0)
    paired = jnp.dot(band.astype(BF16), own, preferred_element_type=F32)
    edge = lax.broadcasted_iota(jnp.int32, (1, HALO), 1)
    band_low = jnp.where(target_col == edge - HALO, live, 0.0)
    paired += jnp.dot(band_low.astype(BF16), emb_ext[0:HALO, :], preferred_element_type=F32)
    nextm.wait_recv()
    next_off = meta_next[0:1, 0:HALO]
    next_live = jnp.where(jnp.logical_and(has_high, edge < meta_next[1:2, 0:HALO]), 1.0, 0.0)
    band_high = jnp.where(rows + edge - next_off == col, next_live, 0.0)
    paired += jnp.dot(band_high.astype(BF16), emb_ext[HALO + rows :, :], preferred_element_type=F32)

    for copy in mpools:
        copy.wait_recv()

    def count_of(m):
        return own_count if m == 0 else meta_pool[m - 1, 1:2, 0:1]

    diag = col == row

    def scored(a_block, m):
        s = lax.dot_general(a_block, pool[m], (((1,), (1,)), ((), ())), preferred_element_type=F32)
        return jnp.exp(2.0 * s - 2.0)

    def summed(x, m):
        return jnp.sum(jnp.where(row < count_of(m), x, 0.0), axis=1, keepdims=True)

    x0 = jnp.where(diag, 0.0, scored(own, 0))
    xs[0] = x0.astype(BF16)
    denom = summed(x0, 0)
    for copy in pools:
        copy.wait_recv()
    for m in range(1, n_batch):
        x = scored(own, m)
        xs[m] = x.astype(BF16)
        denom += summed(x, m)

    def set_rhs(a, a_live, a_denom):
        block = pool[a].astype(F32) * a_live
        rhs[a, :, 0:LANES] = block.astype(BF16)
        rhs[a, :, LANES : 2 * LANES] = (block / a_denom).astype(BF16)

    set_rhs(0, live, denom)
    if n_batch == 2:
        other_denom = summed(scored(pool[1], 0), 0)
        other_denom += summed(jnp.where(diag, 0.0, scored(pool[1], 1)), 1)
        set_rhs(1, (col < count_of(1)).astype(F32), other_denom)
    else:
        def one(a, carry):
            block = pool[a]
            den = jnp.zeros((rows, 1), F32)
            for m in range(n_batch):
                den += summed(jnp.where(jnp.logical_and(diag, a == m), 0.0, scored(block, m)), m)
            a_count = meta_pool[a - 1][1:2, 0:1]
            set_rhs(a, (col < a_count).astype(F32), den)
            return carry

        lax.fori_loop(1, n_batch, one, 0)
    acc = jnp.dot(xs[0], rhs[0], preferred_element_type=F32)
    for m in range(1, n_batch):
        acc += jnp.dot(xs[m], rhs[m], preferred_element_type=F32)
    unit = unit_s[HALO : HALO + rows, :]
    scale = scale_s[HALO : HALO + rows, :]
    grad_unit = 2.0 * (live * (acc[:, 0:LANES] / denom + acc[:, LANES:]) - paired)
    along = jnp.sum(unit * grad_unit, axis=1, keepdims=True)
    gf = ((grad_unit - unit * along) * scale).astype(BF16)
    gh = lax.dot_general(gf, proj_ref[...], (((1,), (1,)), ((), ())), preferred_element_type=F32)
    gp = (gh * slope[HALO : HALO + rows, :]).astype(BF16)
    gt[...] = jnp.transpose(gp)

    def put(owner, c, value):
        if piece % 16 == 0:
            grads[owner, c] = jnp.swapaxes(
                value.astype(BF16).reshape(n_tm, n_batch, piece, LANES), 0, 1
            )
        else:
            tmp[...] = value
            for i in range(n_tm):
                for j in range(n_batch):
                    at = i * share + j * piece
                    grads[owner, c, j, i] = tmp[at : at + piece, :].astype(BF16)

    reps = {}

    def produce(c):
        if c < chunks - 1:
            value = jnp.dot(
                gt[...], taps[HALO : HALO + rows, 2 * c * LANES : 2 * (c + 1) * LANES], preferred_element_type=F32
            )
            put(0, c, value[:, 0:LANES])
            put(1, c, value[:, LANES:])
        else:
            put(0, c, lax.dot_general(
                hid2[HALO : HALO + rows, :], gf, (((0,), (0,)), ((), ())), preferred_element_type=F32
            ))
            put(1, c, jnp.dot(gt[...], jnp.ones((rows, LANES), BF16), preferred_element_type=F32))
        reps[c] = send(grads.at[other, c], rep_in.at[c], rep_sem, (c,), {"rep": other})

    bats, tms, gats, fins = {}, {}, {}, {}

    def over_batch(c):
        reps[c].wait_recv()
        part_one[c] = (grads[r, c].astype(F32) + rep_in[c].astype(F32)).astype(BF16)
        bats[c] = [
            send(part_one.at[c, lax.rem(b + o, n_batch)], batch_in.at[c, o - 1], batch_sem, (c, o - 1), batch_at(o))
            for o in range(1, n_batch)
        ]

    def over_tm(c):
        value = part_one[c, b].astype(F32)
        for o in range(1, n_batch):
            bats[c][o - 1].wait_recv()
            value += batch_in[c, o - 1].astype(F32)
        part_two[c] = value.astype(BF16)
        tms[c] = [
            send(part_two.at[c, lax.rem(z + o, n_tm)], tm_in.at[c, o - 1], tm_sem, (c, o - 1), tm_at(o))
            for o in range(1, n_tm)
        ]

    def finish(c):
        value = part_two[c, z].astype(F32)
        for o in range(1, n_tm):
            tms[c][o - 1].wait_recv()
            value += tm_in[c, o - 1].astype(F32)
        final[r, c, b] = value.astype(BF16)
        gats[c] = [
            send(final.at[r, c, b], final.at[r, c, b], gat_sem, (c, o - 1), batch_at(o)) for o in range(1, n_batch)
        ]

    def share_out(c):
        for copy in gats[c]:
            copy.wait_recv()
        fins[c] = send(final.at[r, c], final.at[r, c], fin_sem, (c,), {"rep": other})

    def write(c):
        fins[c].wait_recv()
        for owner in range(2):
            sums_out[owner, c] = final[owner, c]

    for c in range(chunks):
        produce(c)
        if c >= 1:
            over_batch(c - 1)
    over_batch(chunks - 1)
    for step in range(chunks + 2):
        if step < chunks:
            over_tm(step)
        if step >= 2:
            finish(step - 2)
    for c in range(chunks):
        share_out(c)
    for c in range(chunks):
        write(c)
    for copy in started:
        copy.wait_send()


def spread(emb_ref, sums_ref, emb_out, conv_out, bias_out, proj_out, tmp):
    chunks, n_batch, piece = sums_ref.shape[1:4]
    per_tap = conv_out.shape[1] // LANES
    share = n_batch * piece
    emb_out[...] = emb_ref[...]
    for c in range(chunks):
        for owner in range(2):
            if piece % 16 == 0:
                value = sums_ref[owner, c].astype(F32).reshape(share, LANES)
            else:
                for j in range(n_batch):
                    tmp[j * piece : (j + 1) * piece, :] = sums_ref[owner, c, j].astype(F32)
                value = tmp[...]
            if c < chunks - 1:
                k, part = divmod(2 * c + owner, per_tap)
                conv_out[k, part * LANES : (part + 1) * LANES, :] = jnp.transpose(value)
            elif owner == 0:
                proj_out[...] = value
            else:
                bias_out[...] = jnp.transpose(value)[0:1, :]


def per_device(
    n_tm, n_batch,
    latents, session_ids, session_gain, session_shift, first_conv_weight, first_conv_bias,
    second_conv_weight, second_conv_bias, proj_weight, offsets, counts,
):
    rows, channels = latents.shape[1:]
    emb = proj_weight.shape[1]
    total = rows + 2 * HALO
    share = channels // n_tm
    piece = share // n_batch
    chunks = (3 * channels // LANES + 2) // 2
    vmem = pl.BlockSpec(memory_space=pltpu.VMEM)
    hbm = pl.BlockSpec(memory_space=pl.ANY)
    nb = n_batch - 1
    dma = pltpu.SemaphoreType.DMA
    id_count = jnp.where(
        lax.broadcasted_iota(jnp.int32, (8, LANES), 0) == 0, session_ids[0], counts[0, 0]
    )
    embed, sums = pl.pallas_call(
        functools.partial(kernel, n_tm, n_batch, chunks),
        out_shape=(
            jax.ShapeDtypeStruct((rows, emb), BF16),
            jax.ShapeDtypeStruct((2, chunks, n_batch, piece, LANES), BF16),
        ),
        in_specs=[vmem, vmem, vmem, vmem, hbm, vmem, hbm, vmem, vmem, vmem],
        out_specs=(vmem, vmem),
        scratch_shapes=[
            pltpu.VMEM((3 * channels, channels), BF16),
            pltpu.VMEM((3 * channels, channels), BF16),
            dma((2,)),
            pltpu.VMEM((2, HALO, channels), BF16),
            pltpu.VMEM((8, LANES), jnp.int32),
            pltpu.VMEM((8, LANES), jnp.int32),
            pltpu.VMEM((nb, 8, LANES), jnp.int32),
            pltpu.VMEM((total + 2 * PAD, channels), F32),
            pltpu.VMEM((total, 3 * channels), BF16),
            pltpu.VMEM((total, channels), F32),
            pltpu.VMEM((total, channels), F32),
            pltpu.VMEM((total, channels), BF16),
            pltpu.VMEM((total, emb), F32),
            pltpu.VMEM((total, LANES), F32),
            pltpu.VMEM((total, emb), BF16),
            pltpu.VMEM((n_batch, rows, emb), BF16),
            pltpu.VMEM((n_batch, rows, rows), BF16),
            pltpu.VMEM((n_batch, rows, 2 * emb), BF16),
            pltpu.VMEM((channels, rows), BF16),
            pltpu.VMEM((2, chunks, n_batch, n_tm, piece, LANES), BF16),
            pltpu.VMEM((chunks, n_batch, n_tm, piece, LANES), BF16),
            pltpu.VMEM((chunks, n_batch, n_tm, piece, LANES), BF16),
            pltpu.VMEM((chunks, nb, n_tm, piece, LANES), BF16),
            pltpu.VMEM((chunks, n_tm, piece, LANES), BF16),
            pltpu.VMEM((chunks, n_tm - 1, piece, LANES), BF16),
            pltpu.VMEM((2, chunks, n_batch, piece, LANES), BF16),
            pltpu.VMEM((channels, LANES), F32),
            dma((2, 2)),
            dma((2, 1)),
            dma((2, nb)),
            dma((2, nb)),
            dma((2, chunks)),
            dma((2, chunks, nb)),
            dma((2, chunks, n_tm - 1)),
            dma((2, chunks, nb)),
            dma((2, chunks)),
        ],
        compiler_params=pltpu.CompilerParams(
            collective_id=0, has_side_effects=True, vmem_limit_bytes=56 * 1024 * 1024
        ),
    )(
        id_count, latents[0], session_gain, session_shift,
        first_conv_weight.reshape(3 * channels, channels), first_conv_bias[None],
        second_conv_weight.reshape(3 * channels, channels), second_conv_bias[None],
        proj_weight, offsets,
    )
    embed, conv, bias, proj = pl.pallas_call(
        spread,
        out_shape=(
            jax.ShapeDtypeStruct((rows, emb), BF16),
            jax.ShapeDtypeStruct((3, channels, share), F32),
            jax.ShapeDtypeStruct((1, share), F32),
            jax.ShapeDtypeStruct((share, emb), F32),
        ),
        in_specs=[vmem, vmem],
        out_specs=(vmem, vmem, vmem, vmem),
        scratch_shapes=[pltpu.VMEM((share, LANES), F32)],
    )(embed, sums)
    return embed[None], conv, bias[0], proj


def solution(mesh):
    return jax.shard_map(
        functools.partial(per_device, mesh.shape["tm"], mesh.shape["batch"]),
        mesh=mesh,
        in_specs=(
            P(("groups", "batch", "rep"), "tm", None),
            P(("groups", "batch", "rep")),
            P(),
            P(),
            P(),
            P(),
            P(),
            P(),
            P(),
            P(("groups", "batch", "rep"), "tm"),
            P(("groups", "batch", "rep"), "tm"),
        ),
        out_specs=(
            P(("groups", "batch", "rep"), "tm", None),
            P("groups", None, "tm"),
            P(("groups", "tm")),
            P(("groups", "tm"), None),
        ),
        check_vma=False,
    )
```

```python
import functools

import jax
import jax.numpy as jnp
from jax import lax
from jax.experimental import pallas as pl
from jax.experimental.pallas import tpu as pltpu
from jax.sharding import PartitionSpec as P

OFF_MAX = 10
HALO = 16
PAD = 8
LANES = 128
F32 = jnp.float32
BF16 = jnp.bfloat16
GELU_C = 0.7978845608028654
GELU_A = 0.044715


def gelu_parts(x):
    square = x * x
    th = jnp.tanh(GELU_C * x * (1.0 + GELU_A * square))
    half = 0.5 * (1.0 + th)
    slope = half + (0.5 * GELU_C) * x * (1.0 - th * th) * (1.0 + (3.0 * GELU_A) * square)
    return x * half, slope


def kernel(
    n_tm, n_batch, chunks,
    id_count_ref, lat_ref, gain_ref, shift_ref, w1_hbm, b1_ref, w2_hbm, b2_ref, proj_ref, off_ref,
    emb_out, sums_out,
    w1, w2, wsem, halo, meta, meta_next, meta_pool, ext, taps, pre, slope, hid2, unit_s, scale_s, emb_ext, pool,
    xs, rhs, gt, grads, rep_in, part_one, batch_in, part_two, tm_in, final, tmp, zf_in, zf_sum, zf_batch,
    halo_sem, meta_sem, mpool_sem, pool_sem, rep_sem, batch_sem, tm_sem, gat_sem, fin_sem, zf_sem, zf_batch_sem,
):
    rows, channels = lat_ref.shape
    total = rows + 2 * HALO
    share = channels // n_tm
    piece = share // n_batch
    z = lax.axis_index("tm")
    b = lax.axis_index("batch")
    r = lax.axis_index("rep")
    other = 1 - r
    load1 = pltpu.make_async_copy(w1_hbm, w1, wsem.at[0])
    load2 = pltpu.make_async_copy(w2_hbm, w2, wsem.at[1])
    load1.start()
    load2.start()
    meta[0:1, :] = off_ref[0:1, 0:LANES]
    meta[1:2, :] = id_count_ref[1:2, :]
    meta[2:8, :] = jnp.zeros((6, LANES), jnp.int32)

    barrier = pltpu.get_barrier_semaphore()

    def tm_at(o):
        return {"tm": lax.rem(z + o, n_tm)}

    def batch_at(o):
        return {"batch": lax.rem(b + o, n_batch)}

    peers = [tm_at(o) for o in range(1, n_tm)] + [batch_at(o) for o in range(1, n_batch)] + [{"rep": other}]
    for peer in peers:
        pl.semaphore_signal(barrier, inc=1, device_id=peer, device_id_type=pl.DeviceIdType.MESH)
    pl.semaphore_wait(barrier, len(peers))

    started = []

    def send(src, dst, sems, index, peer):
        copy = pltpu.make_async_remote_copy(
            src_ref=src, dst_ref=dst, send_sem=sems.at[(0,) + index], recv_sem=sems.at[(1,) + index],
            device_id=peer, device_id_type=pl.DeviceIdType.MESH,
        )
        copy.start()
        started.append(copy)
        return copy

    low = send(lat_ref.at[pl.ds(rows - HALO, HALO)], halo.at[0], halo_sem, (0,), tm_at(1))
    high = send(lat_ref.at[pl.ds(0, HALO)], halo.at[1], halo_sem, (1,), tm_at(n_tm - 1))
    nextm = send(meta, meta_next, meta_sem, (0,), tm_at(n_tm - 1))
    mpools = [send(meta, meta_pool.at[o - 1], mpool_sem, (o - 1,), batch_at(o)) for o in range(1, n_batch)]

    pick = lax.broadcasted_iota(jnp.int32, gain_ref.shape, 0) == id_count_ref[0:1, 0:1]
    gain = jnp.sum(jnp.where(pick, gain_ref[...], 0.0), axis=0, keepdims=True)
    shift = jnp.sum(jnp.where(pick, shift_ref[...], 0.0), axis=0, keepdims=True)

    def based(block):
        return (block.astype(F32) * gain + shift).astype(BF16).astype(F32)

    ext[0:PAD, :] = jnp.zeros((PAD, channels), F32)
    ext[PAD + total :, :] = jnp.zeros((PAD, channels), F32)
    ext[PAD + HALO : PAD + HALO + rows, :] = based(lat_ref[...])
    ext[PAD : PAD + HALO, :] = jnp.zeros((HALO, channels), F32)
    ext[PAD + HALO + rows : PAD + total, :] = jnp.zeros((HALO, channels), F32)
    has_low = z > 0
    has_high = z < n_tm - 1
    half = total // 2
    starts = (0, half)
    edge_rows = 2 * HALO
    middle = total - 2 * edge_rows

    def gather_taps(dilation, begin, count):
        for k in range(3):
            first = PAD + begin + (k - 1) * dilation
            taps[begin : begin + count, k * channels : (k + 1) * channels] = ext[first : first + count, :].astype(BF16)

    def first_hidden(begin, count):
        x = pre[begin : begin + count, :] + b1_ref[...]
        value = 0.5 * x * (1.0 + jnp.tanh(GELU_C * x * (1.0 + GELU_A * x * x)))
        hid = (ext[PAD + begin : PAD + begin + count, :] + value).astype(BF16).astype(F32)
        at = begin + lax.broadcasted_iota(jnp.int32, (count, 1), 0)
        inside = jnp.logical_and(
            jnp.logical_or(has_low, at >= HALO), jnp.logical_or(has_high, at < HALO + rows)
        )
        return jnp.where(inside, hid, 0.0)

    gather_taps(1, edge_rows, middle)
    load1.wait()
    pre[edge_rows : edge_rows + middle, :] = jnp.dot(
        taps[edge_rows : edge_rows + middle, :], w1[...], preferred_element_type=F32
    )
    low.wait_recv()
    high.wait_recv()
    ext[PAD : PAD + HALO, :] = jnp.where(has_low, based(halo[0]), 0.0)
    ext[PAD + HALO + rows : PAD + total, :] = jnp.where(has_high, based(halo[1]), 0.0)
    last = total - edge_rows
    gather_taps(1, 0, edge_rows)
    gather_taps(1, last, edge_rows)
    ends = jnp.concatenate([taps[0:edge_rows, :], taps[last:, :]], axis=0)
    ends = jnp.dot(ends, w1[...], preferred_element_type=F32)
    pre[0:edge_rows, :] = ends[0:edge_rows, :]
    pre[last:, :] = ends[edge_rows:, :]
    for s in starts:
        ext[PAD + s : PAD + s + half, :] = first_hidden(s, half)
    gather_taps(2, 0, total)
    load2.wait()
    for s in starts:
        pre[s : s + half, :] = jnp.dot(taps[s : s + half, :], w2[...], preferred_element_type=F32)
    for s in starts:
        value, deriv = gelu_parts(pre[s : s + half, :] + b2_ref[...])
        slope[s : s + half, :] = deriv
        hid = (ext[PAD + s : PAD + s + half, :] + value).astype(BF16)
        hid2[s : s + half, :] = hid
        feats = jnp.dot(hid, proj_ref[...], preferred_element_type=F32)
        scale = lax.rsqrt(jnp.sum(feats * feats, axis=1, keepdims=True) + 1e-06)
        unit = feats * scale
        unit_s[s : s + half, :] = unit
        scale_s[s : s + half, :] = jnp.broadcast_to(scale, (half, LANES))
        emb_ext[s : s + half, :] = unit.astype(BF16)
    own = emb_ext[HALO : HALO + rows, :]
    emb_out[...] = own
    pool[0] = own
    pools = [send(pool.at[0], pool.at[o], pool_sem, (o - 1,), batch_at(o)) for o in range(1, n_batch)]

    own_count = meta[1:2, 0:1]
    col = lax.broadcasted_iota(jnp.int32, (rows, 1), 0)
    row = lax.broadcasted_iota(jnp.int32, (1, rows), 1)
    live = (col < own_count).astype(F32)
    first = z * rows
    offs_row = off_ref[...]
    offs_col = jnp.transpose(jnp.broadcast_to(offs_row.astype(F32), (LANES, rows)))[:, 0:1].astype(jnp.int32)
    target_col = jnp.where(first + col - offs_col >= 0, col - offs_col, col + offs_col)
    target_row = jnp.where(first + row - offs_row >= 0, row - offs_row, row + offs_row)
    live_row = (row < own_count).astype(F32)
    band = jnp.where(target_col == row, live, 0.0) + jnp.where(target_row == col, live_row, 0.0)
    paired = jnp.dot(band.astype(BF16), own, preferred_element_type=F32)
    edge = lax.broadcasted_iota(jnp.int32, (1, HALO), 1)
    band_low = jnp.where(target_col == edge - HALO, live, 0.0)
    paired += jnp.dot(band_low.astype(BF16), emb_ext[0:HALO, :], preferred_element_type=F32)
    nextm.wait_recv()
    next_off = meta_next[0:1, 0:HALO]
    next_live = jnp.where(jnp.logical_and(has_high, edge < meta_next[1:2, 0:HALO]), 1.0, 0.0)
    band_high = jnp.where(rows + edge - next_off == col, next_live, 0.0)
    paired += jnp.dot(band_high.astype(BF16), emb_ext[HALO + rows :, :], preferred_element_type=F32)

    for copy in mpools:
        copy.wait_recv()

    def count_of(m):
        return own_count if m == 0 else meta_pool[m - 1, 1:2, 0:1]

    diag = col == row

    def scored(a_block, m):
        s = lax.dot_general(a_block, pool[m], (((1,), (1,)), ((), ())), preferred_element_type=F32)
        return jnp.exp(2.0 * s - 2.0)

    def summed(x, m):
        return jnp.sum(jnp.where(row < count_of(m), x, 0.0), axis=1, keepdims=True)

    x0 = jnp.where(diag, 0.0, scored(own, 0))
    xs[0] = x0.astype(BF16)
    denom = summed(x0, 0)
    for copy in pools:
        copy.wait_recv()
    for m in range(1, n_batch):
        x = scored(own, m)
        xs[m] = x.astype(BF16)
        denom += summed(x, m)

    def set_rhs(a, a_live, a_denom):
        block = pool[a].astype(F32) * a_live
        rhs[a, :, 0:LANES] = block.astype(BF16)
        rhs[a, :, LANES : 2 * LANES] = (block / a_denom).astype(BF16)

    set_rhs(0, live, denom)
    if n_batch == 2:
        other_denom = summed(scored(pool[1], 0), 0)
        other_denom += summed(jnp.where(diag, 0.0, scored(pool[1], 1)), 1)
        set_rhs(1, (col < count_of(1)).astype(F32), other_denom)
    else:
        def one(a, carry):
            block = pool[a]
            den = jnp.zeros((rows, 1), F32)
            for m in range(n_batch):
                den += summed(jnp.where(jnp.logical_and(diag, a == m), 0.0, scored(block, m)), m)
            a_count = meta_pool[a - 1][1:2, 0:1]
            set_rhs(a, (col < a_count).astype(F32), den)
            return carry

        lax.fori_loop(1, n_batch, one, 0)
    acc = jnp.dot(xs[0], rhs[0], preferred_element_type=F32)
    for m in range(1, n_batch):
        acc += jnp.dot(xs[m], rhs[m], preferred_element_type=F32)
    unit = unit_s[HALO : HALO + rows, :]
    scale = scale_s[HALO : HALO + rows, :]
    grad_unit = 2.0 * (live * (acc[:, 0:LANES] / denom + acc[:, LANES:]) - paired)
    along = jnp.sum(unit * grad_unit, axis=1, keepdims=True)
    gf = ((grad_unit - unit * along) * scale).astype(BF16)
    gh = lax.dot_general(gf, proj_ref[...], (((1,), (1,)), ((), ())), preferred_element_type=F32)
    gp = (gh * slope[HALO : HALO + rows, :]).astype(BF16)
    gt[...] = jnp.transpose(gp)

    def put(owner, c, value):
        if piece % 16 == 0:
            grads[owner, c] = jnp.swapaxes(
                value.astype(BF16).reshape(n_tm, n_batch, piece, LANES), 0, 1
            )
        else:
            tmp[...] = value
            for i in range(n_tm):
                for j in range(n_batch):
                    at = i * share + j * piece
                    grads[owner, c, j, i] = tmp[at : at + piece, :].astype(BF16)

    reps = {}

    def produce(c):
        if c < chunks - 1:
            value = jnp.dot(
                gt[...], taps[HALO : HALO + rows, 2 * c * LANES : 2 * (c + 1) * LANES], preferred_element_type=F32
            )
            put(0, c, value[:, 0:LANES])
            put(1, c, value[:, LANES:])
        else:
            put(0, c, lax.dot_general(
                hid2[HALO : HALO + rows, :], gf, (((0,), (0,)), ((), ())), preferred_element_type=F32
            ))
            put(1, c, jnp.dot(gt[...], jnp.ones((rows, LANES), BF16), preferred_element_type=F32))
        reps[c] = send(grads.at[other, c], rep_in.at[c], rep_sem, (c,), {"rep": other})

    bats, tms, gats, fins = {}, {}, {}, {}

    def over_batch(c):
        reps[c].wait_recv()
        part_one[c] = (grads[r, c].astype(F32) + rep_in[c].astype(F32)).astype(BF16)
        bats[c] = [
            send(part_one.at[c, lax.rem(b + o, n_batch)], batch_in.at[c, o - 1], batch_sem, (c, o - 1), batch_at(o))
            for o in range(1, n_batch)
        ]

    def over_tm(c):
        value = part_one[c, b].astype(F32)
        for o in range(1, n_batch):
            bats[c][o - 1].wait_recv()
            value += batch_in[c, o - 1].astype(F32)
        part_two[c] = value.astype(BF16)
        tms[c] = [
            send(part_two.at[c, lax.rem(z + o, n_tm)], tm_in.at[c, o - 1], tm_sem, (c, o - 1), tm_at(o))
            for o in range(1, n_tm)
        ]

    def finish(c):
        value = part_two[c, z].astype(F32)
        for o in range(1, n_tm):
            tms[c][o - 1].wait_recv()
            value += tm_in[c, o - 1].astype(F32)
        final[r, c, b] = value.astype(BF16)
        gats[c] = [
            send(final.at[r, c, b], final.at[r, c, b], gat_sem, (c, o - 1), batch_at(o)) for o in range(1, n_batch)
        ]

    def share_out(c):
        for copy in gats[c]:
            copy.wait_recv()
        fins[c] = send(final.at[r, c], final.at[r, c], fin_sem, (c,), {"rep": other})

    def write(c):
        fins[c].wait_recv()
        for owner in range(2):
            sums_out[owner, c] = final[owner, c]

    def tm_first(c):
        reps[c].wait_recv()
        part_one[c] = (grads[r, c].astype(F32) + rep_in[c].astype(F32)).astype(BF16)
        tms[c] = [
            send(part_one.at[c, :, lax.rem(z + o, n_tm)], zf_in.at[o - 1], zf_sem, (o - 1,), tm_at(o))
            for o in range(1, n_tm)
        ]

    def then_batch(c):
        value = part_one[c, :, z].astype(F32)
        for o in range(1, n_tm):
            tms[c][o - 1].wait_recv()
            value += zf_in[o - 1].astype(F32)
        zf_sum[...] = value.astype(BF16)
        bats[c] = [
            send(zf_sum.at[lax.rem(b + o, n_batch)], zf_batch.at[o - 1], zf_batch_sem, (o - 1,), batch_at(o))
            for o in range(1, n_batch)
        ]

    def finish_tm_first(c):
        value = zf_sum[b].astype(F32)
        for o in range(1, n_batch):
            bats[c][o - 1].wait_recv()
            value += zf_batch[o - 1].astype(F32)
        final[r, c, b] = value.astype(BF16)
        gats[c] = [
            send(final.at[r, c, b], final.at[r, c, b], gat_sem, (c, o - 1), batch_at(o)) for o in range(1, n_batch)
        ]

    for c in range(chunks):
        produce(c)
        if c == 1:
            tm_first(0)
        elif c > 1:
            over_batch(c - 1)
    over_batch(chunks - 1)
    over_tm(1)
    over_tm(2)
    then_batch(0)
    for step in range(3, chunks + 2):
        if step < chunks:
            over_tm(step)
        finish(step - 2)
    finish_tm_first(0)
    for c in range(chunks):
        share_out(c)
    for c in range(chunks):
        write(c)
    for copy in started:
        copy.wait_send()


def spread(emb_ref, sums_ref, emb_out, conv_out, bias_out, proj_out, tmp):
    chunks, n_batch, piece = sums_ref.shape[1:4]
    per_tap = conv_out.shape[1] // LANES
    share = n_batch * piece
    emb_out[...] = emb_ref[...]
    for c in range(chunks):
        for owner in range(2):
            if piece % 16 == 0:
                value = sums_ref[owner, c].astype(F32).reshape(share, LANES)
            else:
                for j in range(n_batch):
                    tmp[j * piece : (j + 1) * piece, :] = sums_ref[owner, c, j].astype(F32)
                value = tmp[...]
            if c < chunks - 1:
                k, part = divmod(2 * c + owner, per_tap)
                conv_out[k, part * LANES : (part + 1) * LANES, :] = jnp.transpose(value)
            elif owner == 0:
                proj_out[...] = value
            else:
                bias_out[...] = jnp.transpose(value)[0:1, :]


def per_device(
    n_tm, n_batch,
    latents, session_ids, session_gain, session_shift, first_conv_weight, first_conv_bias,
    second_conv_weight, second_conv_bias, proj_weight, offsets, counts,
):
    rows, channels = latents.shape[1:]
    emb = proj_weight.shape[1]
    total = rows + 2 * HALO
    share = channels // n_tm
    piece = share // n_batch
    chunks = (3 * channels // LANES + 2) // 2
    vmem = pl.BlockSpec(memory_space=pltpu.VMEM)
    hbm = pl.BlockSpec(memory_space=pl.ANY)
    nb = n_batch - 1
    dma = pltpu.SemaphoreType.DMA
    id_count = jnp.where(
        lax.broadcasted_iota(jnp.int32, (8, LANES), 0) == 0, session_ids[0], counts[0, 0]
    )
    embed, sums = pl.pallas_call(
        functools.partial(kernel, n_tm, n_batch, chunks),
        out_shape=(
            jax.ShapeDtypeStruct((rows, emb), BF16),
            jax.ShapeDtypeStruct((2, chunks, n_batch, piece, LANES), BF16),
        ),
        in_specs=[vmem, vmem, vmem, vmem, hbm, vmem, hbm, vmem, vmem, vmem],
        out_specs=(vmem, vmem),
        scratch_shapes=[
            pltpu.VMEM((3 * channels, channels), BF16),
            pltpu.VMEM((3 * channels, channels), BF16),
            dma((2,)),
            pltpu.VMEM((2, HALO, channels), BF16),
            pltpu.VMEM((8, LANES), jnp.int32),
            pltpu.VMEM((8, LANES), jnp.int32),
            pltpu.VMEM((nb, 8, LANES), jnp.int32),
            pltpu.VMEM((total + 2 * PAD, channels), F32),
            pltpu.VMEM((total, 3 * channels), BF16),
            pltpu.VMEM((total, channels), F32),
            pltpu.VMEM((total, channels), F32),
            pltpu.VMEM((total, channels), BF16),
            pltpu.VMEM((total, emb), F32),
            pltpu.VMEM((total, LANES), F32),
            pltpu.VMEM((total, emb), BF16),
            pltpu.VMEM((n_batch, rows, emb), BF16),
            pltpu.VMEM((n_batch, rows, rows), BF16),
            pltpu.VMEM((n_batch, rows, 2 * emb), BF16),
            pltpu.VMEM((channels, rows), BF16),
            pltpu.VMEM((2, chunks, n_batch, n_tm, piece, LANES), BF16),
            pltpu.VMEM((chunks, n_batch, n_tm, piece, LANES), BF16),
            pltpu.VMEM((chunks, n_batch, n_tm, piece, LANES), BF16),
            pltpu.VMEM((chunks, nb, n_tm, piece, LANES), BF16),
            pltpu.VMEM((chunks, n_tm, piece, LANES), BF16),
            pltpu.VMEM((chunks, n_tm - 1, piece, LANES), BF16),
            pltpu.VMEM((2, chunks, n_batch, piece, LANES), BF16),
            pltpu.VMEM((channels, LANES), F32),
            pltpu.VMEM((n_tm - 1, n_batch, piece, LANES), BF16),
            pltpu.VMEM((n_batch, piece, LANES), BF16),
            pltpu.VMEM((nb, piece, LANES), BF16),
            dma((2, 2)),
            dma((2, 1)),
            dma((2, nb)),
            dma((2, nb)),
            dma((2, chunks)),
            dma((2, chunks, nb)),
            dma((2, chunks, n_tm - 1)),
            dma((2, chunks, nb)),
            dma((2, chunks)),
            dma((2, n_tm - 1)),
            dma((2, nb)),
        ],
        compiler_params=pltpu.CompilerParams(
            collective_id=0, has_side_effects=True, vmem_limit_bytes=56 * 1024 * 1024
        ),
    )(
        id_count, latents[0], session_gain, session_shift,
        first_conv_weight.reshape(3 * channels, channels), first_conv_bias[None],
        second_conv_weight.reshape(3 * channels, channels), second_conv_bias[None],
        proj_weight, offsets,
    )
    embed, conv, bias, proj = pl.pallas_call(
        spread,
        out_shape=(
            jax.ShapeDtypeStruct((rows, emb), BF16),
            jax.ShapeDtypeStruct((3, channels, share), F32),
            jax.ShapeDtypeStruct((1, share), F32),
            jax.ShapeDtypeStruct((share, emb), F32),
        ),
        in_specs=[vmem, vmem],
        out_specs=(vmem, vmem, vmem, vmem),
        scratch_shapes=[pltpu.VMEM((share, LANES), F32)],
    )(embed, sums)
    return embed[None], conv, bias[0], proj


def solution(mesh):
    return jax.shard_map(
        functools.partial(per_device, mesh.shape["tm"], mesh.shape["batch"]),
        mesh=mesh,
        in_specs=(
            P(("groups", "batch", "rep"), "tm", None),
            P(("groups", "batch", "rep")),
            P(),
            P(),
            P(),
            P(),
            P(),
            P(),
            P(),
            P(("groups", "batch", "rep"), "tm"),
            P(("groups", "batch", "rep"), "tm"),
        ),
        out_specs=(
            P(("groups", "batch", "rep"), "tm", None),
            P("groups", None, "tm"),
            P(("groups", "tm")),
            P(("groups", "tm"), None),
        ),
        check_vma=False,
    )
```
